32 devices in a mesh: vec: 8 (over y, x, core), fld: 4 (over z).
Axes of the slice: x: 2, y: 2, z: 4, core: 2. Of those that a mesh axis runs over, the one named last changes fastest.
Arguments:
- profiles: float32 [1024, 32768], P('vec', 'fld'), may hold values from 0.04 to 21
- pivots: int32 [8, 4], P('vec'), may hold values from 0 to 127
- roles: int32 [8, 3], P('vec'), may hold values from 0 to 2, each once within a row
Outputs:
- pair_means: float32 [8, 128, 3, 128], P('vec', 'fld')
- similarity: float32 [8, 128, 4, 128], P('vec', 'fld')
The draws below stay inside these ranges and needn't reach their ends.
Inputs may be any that keep to these rules, and one draw needn't show every extreme that they name: Each row of roles holds 0, 1 and 2 once each.
All inputs are finite; a program needn't handle non-finite values.
Results may differ from the reference program's by a relative error of at most 0.0003.
Values sent between devices are 32-bit elements; how exact they have to be, the bound alone decides.
A program may use at most 128 MiB of HBM per device.

```python
import jax
import jax.numpy as jnp
from jax import lax

FIELDS = 32768
BS = 128
PIVOTS = 4
VECTORS = 1024
N_VEC = 8


factor_count = 64


def draw_profiles(key, part):
    key_weights = jax.random.fold_in(key, 11)
    key_fields = jax.random.fold_in(key, 12)
    key_noise = jax.random.fold_in(key, 13)
    key_level = jax.random.fold_in(key, 14)
    key_spread = jax.random.fold_in(key, 15)
    raw = jax.random.normal(key_weights, (VECTORS, factor_count), jnp.float32)
    weights = raw * raw * raw
    weights = weights / jnp.sqrt(jnp.sum(weights * weights, axis=1, keepdims=True) + 1e-06)
    level = jax.random.uniform(key_level, (VECTORS, 1), jnp.float32, -2.0, 2.0)
    patterns = jax.random.normal(key_fields, (factor_count, FIELDS), jnp.float32)
    noise = jax.random.normal(key_noise, (VECTORS, FIELDS), jnp.float32)
    spread = jax.random.uniform(key_spread, (VECTORS, 1), jnp.float32, 0.8, 1.2)
    shared = jnp.dot(weights, patterns, precision=lax.Precision.HIGHEST)
    logs = level + spread * (0.85 * shared + 0.53 * noise)
    return jnp.exp(jnp.clip(logs, -3.0, 3.0)).astype(jnp.float32)


def plant(values, key, low, largest):
    shape = values.shape
    place = [jax.random.randint(jax.random.fold_in(key, axis), (), 0, shape[axis]) for axis in range(len(shape))]
    values = values.at[tuple(place)].set(low)
    longest = shape.index(max(shape))
    place[longest] = (place[longest] + 1) % shape[longest]
    return values.at[tuple(place)].set(largest)


def setup_inputs(seed: int = 0) -> dict:
    streams_of = jax.random.split(jax.random.key(seed), 4)
    profiles = draw_profiles(jax.random.fold_in(streams_of[3], 71), 0)
    pivots = plant(jax.random.randint(streams_of[1], (N_VEC, PIVOTS), 0, BS), jax.random.fold_in(streams_of[1], 1), 0, BS - 1).astype(jnp.int32)
    roles = jax.vmap(lambda own: jax.random.permutation(own, 3))(jax.random.split(streams_of[2], N_VEC)).reshape((N_VEC, 3)).astype(jnp.int32)
    return dict(profiles=profiles, pivots=pivots, roles=roles)


def min_sums(left_rows, right_rows, group_size):
    total = left_rows.shape[0]
    stacked = left_rows.reshape(total // group_size, group_size, left_rows.shape[1])

    def block_sum(part_rows):
        return jnp.sum(jnp.minimum(part_rows[:, None, :], right_rows[None, :, :]), axis=2)

    return lax.map(block_sum, stacked).reshape(total, right_rows.shape[0])


def reference(profiles, pivots, roles):
    stride = N_VEC // 8
    blocks = profiles.reshape(N_VEC, BS, FIELDS)
    field_scale = 1.0 / FIELDS

    def per_block(block_index):
        own_block = blocks[block_index]
        near_block = blocks[(block_index - stride) % N_VEC]
        far_block = blocks[(block_index - 2 * stride) % N_VEC]
        stacked = jnp.stack([own_block, near_block, far_block])
        lead_block = stacked[roles[block_index, 0]]
        pivot_block = stacked[roles[block_index, 1]]
        tail_block = stacked[roles[block_index, 2]]
        chosen = pivots[block_index]
        pair_tables = jnp.stack([min_sums(lead_block, pivot_block, 4), min_sums(lead_block, tail_block, 4), min_sums(pivot_block, tail_block, 4)], 1) * field_scale
        pivot_vectors = pivot_block[chosen]
        crossed = jnp.minimum(pivot_vectors[:, None, :], tail_block[None, :, :]).reshape(PIVOTS * BS, FIELDS)
        triple = min_sums(lead_block, crossed, 4).reshape(BS, PIVOTS, BS) * field_scale
        first_cols = jnp.take(pair_tables[:, 0, :], chosen, axis=1)
        pivot_rows = pair_tables[:, 2, :][chosen]
        similar = (first_cols[:, :, None] + pair_tables[:, 1, :][:, None, :] + pivot_rows[None, :, :] - triple) * 0.5
        return pair_tables, similar

    pair_means, similarity = lax.map(per_block, jnp.arange(N_VEC, dtype=jnp.int32))
    return pair_means, similarity
```

```python
import functools

import jax
import jax.numpy as jnp
from jax import lax
from jax.experimental import pallas as pl
from jax.experimental.pallas import tpu as pltpu
from jax.sharding import PartitionSpec as P

FIELDS = 32768
CHUNKS = 2
LANES = 128
SUB = 8


def shifted(shard, axis, by):
    peers = lax.axis_size(axis)
    return lax.ppermute(shard, axis, [(i, (i + by) % peers) for i in range(peers)])


def table_kernel(unroll, roles, pivots, own, near, far, out, held, piv, sems):
    rows, width = own.shape
    count = piv.shape[0]
    steps = width // LANES
    copies = [
        pltpu.make_async_copy(block, held.at[i], sems.at[i])
        for i, block in enumerate((own, near, far))
    ]
    for copy in copies:
        copy.start()
    for copy in copies:
        copy.wait()
    first, middle, last = roles[0], roles[1], roles[2]

    def tile(which, row, col):
        return held[which, pl.ds(pl.multiple_of(row, SUB), SUB), pl.ds(pl.multiple_of(col, LANES), LANES)]

    sub_id = lax.broadcasted_iota(jnp.int32, (SUB, LANES), 0)
    lane_id = lax.broadcasted_iota(jnp.int32, (SUB, LANES), 1)
    for m in range(count):
        base = (pivots[m] // SUB) * SUB
        keep = sub_id == pivots[m] - base

        def spread(step, carry, m=m, base=base, keep=keep):
            col = step * LANES
            value = jnp.sum(jnp.where(keep, tile(middle, base, col), 0.0), axis=0, keepdims=True)
            piv[m, :, pl.ds(pl.multiple_of(col, LANES), LANES)] = jnp.broadcast_to(value, (SUB, LANES))
            return carry

        lax.fori_loop(0, steps, spread, 0)

    def store(table, row, col, sums):
        where = pl.ds(pl.multiple_of(row, SUB), SUB)
        current = out[table, where, :]
        for j, acc in enumerate(sums):
            total = jnp.sum(acc, axis=1, keepdims=True)
            current = jnp.where(lane_id == col + j, total, current)
        out[table, where, :] = current

    def triple_block(index, carry):
        row = (index // (rows // SUB)) * SUB
        col = (index % (rows // SUB)) * SUB

        def step(k, accs):
            at = k * LANES
            lead = tile(first, row, at)
            tail = tile(last, col, at)
            points = [piv[m, :, pl.ds(pl.multiple_of(at, LANES), LANES)] for m in range(count)]
            new = []
            for j in range(SUB):
                both = jnp.minimum(lead, jnp.broadcast_to(tail[j : j + 1], (SUB, LANES)))
                new.append(accs[j * (count + 1)] + both)
                for m in range(count):
                    new.append(accs[j * (count + 1) + 1 + m] + jnp.minimum(both, points[m]))
            return tuple(new)

        zero = jnp.zeros((SUB, LANES), jnp.float32)
        accs = lax.fori_loop(0, steps, step, (zero,) * (SUB * (count + 1)), unroll=unroll)
        store(1, row, col, accs[0 :: count + 1])
        for m in range(count):
            store(3 + m, row, col, accs[1 + m :: count + 1])
        return carry

    lax.fori_loop(0, (rows // SUB) ** 2, triple_block, 0)

    def pair_table(table, left, right):
        group = 4 if rows % (4 * SUB) == 0 else 1

        def pair_block(index, carry):
            row = (index // (rows // SUB)) * SUB * group
            col = (index % (rows // SUB)) * SUB

            def step(k, accs):
                at = k * LANES
                leads = [tile(left, row + g * SUB, at) for g in range(group)]
                tail = tile(right, col, at)
                new = []
                for j in range(SUB):
                    spread = jnp.broadcast_to(tail[j : j + 1], (SUB, LANES))
                    for g in range(group):
                        new.append(accs[j * group + g] + jnp.minimum(leads[g], spread))
                return tuple(new)

            zero = jnp.zeros((SUB, LANES), jnp.float32)
            accs = lax.fori_loop(0, steps, step, (zero,) * (SUB * group), unroll=unroll)
            for g in range(group):
                store(table, row + g * SUB, col, accs[g::group])
            return carry

        lax.fori_loop(0, (rows // SUB) * (rows // SUB // group), pair_block, 0)

    pair_table(0, first, middle)
    pair_table(2, middle, last)


def partial_tables(roles, pivots, own, near, far):
    rows, width = own.shape
    count = pivots.shape[0]
    smem = pl.BlockSpec(memory_space=pltpu.SMEM)
    hbm = pl.BlockSpec(memory_space=pl.ANY)
    pairs = (3 + count) * rows * rows * width
    return pl.pallas_call(
        functools.partial(table_kernel, 2),
        out_shape=jax.ShapeDtypeStruct((3 + count, rows, rows), jnp.float32),
        in_specs=[smem, smem, hbm, hbm, hbm],
        out_specs=pl.BlockSpec(memory_space=pltpu.VMEM),
        scratch_shapes=[
            pltpu.VMEM((3, rows, width), jnp.float32),
            pltpu.VMEM((count, SUB, width), jnp.float32),
            pltpu.SemaphoreType.DMA((3,)),
        ],
        compiler_params=pltpu.CompilerParams(vmem_limit_bytes=40 << 20),
        cost_estimate=pl.CostEstimate(
            flops=2 * pairs, bytes_accessed=3 * rows * width * 4, transcendentals=0
        ),
    )(roles, pivots, own, near, far)


def body(profiles, pivots, roles):
    stride = lax.axis_size("vec") // 8
    n = lax.axis_size("fld")
    width, fields = profiles.shape
    count_piv = pivots.shape[1]
    row_count = width // n
    chosen = pivots[0]
    chunks = CHUNKS if fields % (CHUNKS * LANES) == 0 else 1
    span = fields // chunks
    tables = None
    for k in range(chunks):
        own = profiles[:, k * span : (k + 1) * span]
        near = shifted(own, "vec", stride)
        far = shifted(own, "vec", 2 * stride)
        part = partial_tables(roles[0], chosen, own, near, far)
        tables = part if tables is None else tables + part

    pivot_part = jnp.take(tables[2], chosen, axis=0)
    me = lax.axis_index("fld")
    total = None
    for by in range(n):
        start = lax.rem(me + by, n) * row_count
        piece = lax.dynamic_slice_in_dim(tables, start, row_count, axis=1)
        piece = piece.reshape((3 + count_piv) * row_count, width)
        piece = jnp.concatenate([piece, pivot_part], 0)
        if by:
            piece = shifted(piece, "fld", by)
        total = piece if total is None else total + piece
    total = total * (1.0 / FIELDS)
    rows = total[: (3 + count_piv) * row_count].reshape(3 + count_piv, row_count, width)
    pivot_rows = total[(3 + count_piv) * row_count :]
    first_cols = jnp.take(rows[0], chosen, axis=1)
    pair_tables = jnp.transpose(rows[:3], (1, 0, 2))
    triple = jnp.transpose(rows[3:], (1, 0, 2))
    similar = (
        first_cols[:, :, None] + pair_tables[:, 1, :][:, None, :] + pivot_rows[None, :, :] - triple
    ) * 0.5
    return (pair_tables[None], similar[None])


def solution(mesh):
    return jax.shard_map(
        body,
        mesh=mesh,
        in_specs=(P("vec", "fld"), P("vec", None), P("vec", None)),
        out_specs=(P("vec", "fld", None, None), P("vec", "fld", None, None)),
        check_vma=False,
    )
```

```python
import functools

import jax
import jax.numpy as jnp
from jax import lax
from jax.experimental import pallas as pl
from jax.experimental.pallas import tpu as pltpu
from jax.sharding import PartitionSpec as P

FIELDS = 32768
FIRST = 4
LANES = 128
SUB = 8
TRIPLE_COLS = 8
PAIR_ROWS = 4
UNROLL = 48


def shifted(shard, axis, by):
    peers = lax.axis_size(axis)
    return lax.ppermute(shard, axis, [(i, (i + by) % peers) for i in range(peers)])


def table_kernel(unroll, roles, pivots, own, near, far, out, held, piv, sems):
    rows, width = own.shape
    count = piv.shape[0]
    steps = width // LANES
    copies = [
        pltpu.make_async_copy(block, held.at[i], sems.at[i])
        for i, block in enumerate((own, near, far))
    ]
    for copy in copies:
        copy.start()
    for copy in copies:
        copy.wait()
    first, middle, last = roles[0], roles[1], roles[2]

    def tile(which, row, col):
        return held[which, pl.ds(pl.multiple_of(row, SUB), SUB), pl.ds(pl.multiple_of(col, LANES), LANES)]

    sub_id = lax.broadcasted_iota(jnp.int32, (SUB, LANES), 0)
    lane_id = lax.broadcasted_iota(jnp.int32, (SUB, LANES), 1)
    for m in range(count):
        base = (pivots[m] // SUB) * SUB
        keep = sub_id == pivots[m] - base

        def spread(step, carry, m=m, base=base, keep=keep):
            col = step * LANES
            value = jnp.sum(jnp.where(keep, tile(middle, base, col), 0.0), axis=0, keepdims=True)
            piv[m, :, pl.ds(pl.multiple_of(col, LANES), LANES)] = jnp.broadcast_to(value, (SUB, LANES))
            return carry

        lax.fori_loop(0, steps, spread, 0)

    def store(table, row, col, sums):
        where = pl.ds(pl.multiple_of(row, SUB), SUB)
        current = out[table, where, :]
        for j, acc in enumerate(sums):
            total = jnp.sum(acc, axis=1, keepdims=True)
            current = jnp.where(lane_id == col + j, total, current)
        out[table, where, :] = current

    def triple_block(index, carry):
        row = (index // (rows // SUB)) * SUB
        col = (index % (rows // SUB)) * SUB
        for half in range(0, SUB, TRIPLE_COLS):

            def step(k, accs, half=half):
                at = k * LANES
                lead = tile(first, row, at)
                tail = tile(last, col, at)
                points = [piv[m, :, pl.ds(pl.multiple_of(at, LANES), LANES)] for m in range(count)]
                new = []
                for j in range(TRIPLE_COLS):
                    end = tail[half + j : half + j + 1]
                    both = jnp.minimum(lead, jnp.broadcast_to(end, (SUB, LANES)))
                    new.append(accs[j * (count + 1)] + both)
                    for m in range(count):
                        new.append(accs[j * (count + 1) + 1 + m] + jnp.minimum(both, points[m]))
                return tuple(new)

            zero = jnp.zeros((SUB, LANES), jnp.float32)
            accs = lax.fori_loop(0, steps, step, (zero,) * (TRIPLE_COLS * (count + 1)), unroll=unroll)
            store(1, row, col + half, accs[0 :: count + 1])
            for m in range(count):
                store(3 + m, row, col + half, accs[1 + m :: count + 1])
        return carry

    lax.fori_loop(0, (rows // SUB) ** 2, triple_block, 0)

    def pair_table(table, left, right):
        group = PAIR_ROWS if rows % (PAIR_ROWS * SUB) == 0 else 1

        def pair_block(index, carry):
            row = (index // (rows // SUB)) * SUB * group
            col = (index % (rows // SUB)) * SUB

            def step(k, accs):
                at = k * LANES
                leads = [tile(left, row + g * SUB, at) for g in range(group)]
                tail = tile(right, col, at)
                new = []
                for j in range(SUB):
                    spread = jnp.broadcast_to(tail[j : j + 1], (SUB, LANES))
                    for g in range(group):
                        new.append(accs[j * group + g] + jnp.minimum(leads[g], spread))
                return tuple(new)

            zero = jnp.zeros((SUB, LANES), jnp.float32)
            accs = lax.fori_loop(0, steps, step, (zero,) * (SUB * group), unroll=unroll)
            for g in range(group):
                store(table, row + g * SUB, col, accs[g::group])
            return carry

        lax.fori_loop(0, (rows // SUB) * (rows // SUB // group), pair_block, 0)

    pair_table(0, first, middle)
    pair_table(2, middle, last)


def partial_tables(roles, pivots, own, near, far):
    rows, width = own.shape
    count = pivots.shape[0]
    smem = pl.BlockSpec(memory_space=pltpu.SMEM)
    hbm = pl.BlockSpec(memory_space=pl.ANY)
    pairs = (3 + count) * rows * rows * width
    return pl.pallas_call(
        functools.partial(table_kernel, min(UNROLL, width // LANES)),
        out_shape=jax.ShapeDtypeStruct((3 + count, rows, rows), jnp.float32),
        in_specs=[smem, smem, hbm, hbm, hbm],
        out_specs=pl.BlockSpec(memory_space=pltpu.VMEM),
        scratch_shapes=[
            pltpu.VMEM((3, rows, width), jnp.float32),
            pltpu.VMEM((count, SUB, width), jnp.float32),
            pltpu.SemaphoreType.DMA((3,)),
        ],
        compiler_params=pltpu.CompilerParams(vmem_limit_bytes=40 << 20),
        cost_estimate=pl.CostEstimate(
            flops=2 * pairs, bytes_accessed=3 * rows * width * 4, transcendentals=0
        ),
    )(roles, pivots, own, near, far)


def body(profiles, pivots, roles):
    stride = lax.axis_size("vec") // 8
    n = lax.axis_size("fld")
    width, fields = profiles.shape
    count_piv = pivots.shape[1]
    row_count = width // n
    chosen = pivots[0]
    cut = max(fields // (FIRST * LANES), 1) * LANES
    spans = ((0, cut), (cut, fields)) if cut < fields else ((0, fields),)
    tables = None
    for begin, end in spans:
        own = profiles[:, begin:end]
        near = shifted(own, "vec", stride)
        far = shifted(own, "vec", 2 * stride)
        part = partial_tables(roles[0], chosen, own, near, far)
        tables = part if tables is None else tables + part

    pivot_part = jnp.take(tables[2], chosen, axis=0)
    me = lax.axis_index("fld")
    total = None
    for by in range(n):
        start = lax.rem(me + by, n) * row_count
        piece = lax.dynamic_slice_in_dim(tables, start, row_count, axis=1)
        piece = piece.reshape((3 + count_piv) * row_count, width)
        piece = jnp.concatenate([piece, pivot_part], 0)
        if by:
            piece = shifted(piece, "fld", by)
        total = piece if total is None else total + piece
    total = total * (1.0 / FIELDS)
    rows = total[: (3 + count_piv) * row_count].reshape(3 + count_piv, row_count, width)
    pivot_rows = total[(3 + count_piv) * row_count :]
    first_cols = jnp.take(rows[0], chosen, axis=1)
    pair_tables = jnp.transpose(rows[:3], (1, 0, 2))
    triple = jnp.transpose(rows[3:], (1, 0, 2))
    similar = (
        first_cols[:, :, None] + pair_tables[:, 1, :][:, None, :] + pivot_rows[None, :, :] - triple
    ) * 0.5
    return (pair_tables[None], similar[None])


def solution(mesh):
    return jax.shard_map(
        body,
        mesh=mesh,
        in_specs=(P("vec", "fld"), P("vec", None), P("vec", None)),
        out_specs=(P("vec", "fld", None, None), P("vec", "fld", None, None)),
        check_vma=False,
    )
```

```python
import functools

import jax
import jax.numpy as jnp
from jax import lax
from jax.experimental import pallas as pl
from jax.experimental.pallas import tpu as pltpu
from jax.sharding import PartitionSpec as P

FIELDS = 32768
FIRST = 4
LANES = 128
SUB = 8
TRIPLE_COLS = 8
PAIR_ROWS = 4
UNROLL = 16


def shifted(shard, axis, by):
    peers = lax.axis_size(axis)
    return lax.ppermute(shard, axis, [(i, (i + by) % peers) for i in range(peers)])


def table_kernel(unroll, roles, pivots, own, near, far, out, held, piv, sems):
    rows, width = own.shape
    count = piv.shape[0]
    steps = width // LANES
    copies = [
        pltpu.make_async_copy(block, held.at[i], sems.at[i])
        for i, block in enumerate((own, near, far))
    ]
    for copy in copies:
        copy.start()
    for copy in copies:
        copy.wait()
    first, middle, last = roles[0], roles[1], roles[2]

    def tile(which, row, col):
        return held[which, pl.ds(pl.multiple_of(row, SUB), SUB), pl.ds(pl.multiple_of(col, LANES), LANES)]

    sub_id = lax.broadcasted_iota(jnp.int32, (SUB, LANES), 0)
    lane_id = lax.broadcasted_iota(jnp.int32, (SUB, LANES), 1)
    for m in range(count):
        base = (pivots[m] // SUB) * SUB
        keep = sub_id == pivots[m] - base

        def spread(step, carry, m=m, base=base, keep=keep):
            col = step * LANES
            value = jnp.sum(jnp.where(keep, tile(middle, base, col), 0.0), axis=0, keepdims=True)
            piv[m, :, pl.ds(pl.multiple_of(col, LANES), LANES)] = jnp.broadcast_to(value, (SUB, LANES))
            return carry

        lax.fori_loop(0, steps, spread, 0)

    def store(table, row, col, sums):
        where = pl.ds(pl.multiple_of(row, SUB), SUB)
        current = out[table, where, :]
        for j, acc in enumerate(sums):
            total = jnp.sum(acc, axis=1, keepdims=True)
            current = jnp.where(lane_id == col + j, total, current)
        out[table, where, :] = current

    def triple_block(index, carry):
        row = (index // (rows // SUB)) * SUB
        col = (index % (rows // SUB)) * SUB
        for half in range(0, SUB, TRIPLE_COLS):

            def step(k, accs, half=half):
                at = k * LANES
                lead = tile(first, row, at)
                tail = tile(last, col, at)
                points = [piv[m, :, pl.ds(pl.multiple_of(at, LANES), LANES)] for m in range(count)]
                new = []
                for j in range(TRIPLE_COLS):
                    end = tail[half + j : half + j + 1]
                    both = jnp.minimum(lead, jnp.broadcast_to(end, (SUB, LANES)))
                    new.append(accs[j * (count + 1)] + both)
                    for m in range(count):
                        new.append(accs[j * (count + 1) + 1 + m] + jnp.minimum(both, points[m]))
                return tuple(new)

            zero = jnp.zeros((SUB, LANES), jnp.float32)
            accs = lax.fori_loop(0, steps, step, (zero,) * (TRIPLE_COLS * (count + 1)), unroll=unroll)
            store(1, row, col + half, accs[0 :: count + 1])
            for m in range(count):
                store(3 + m, row, col + half, accs[1 + m :: count + 1])
        return carry

    lax.fori_loop(0, (rows // SUB) ** 2, triple_block, 0)

    def pair_table(table, left, right):
        group = PAIR_ROWS if rows % (PAIR_ROWS * SUB) == 0 else 1

        def pair_block(index, carry):
            row = (index // (rows // SUB)) * SUB * group
            col = (index % (rows // SUB)) * SUB

            def step(k, accs):
                at = k * LANES
                leads = [tile(left, row + g * SUB, at) for g in range(group)]
                tail = tile(right, col, at)
                new = []
                for j in range(SUB):
                    spread = jnp.broadcast_to(tail[j : j + 1], (SUB, LANES))
                    for g in range(group):
                        new.append(accs[j * group + g] + jnp.minimum(leads[g], spread))
                return tuple(new)

            zero = jnp.zeros((SUB, LANES), jnp.float32)
            accs = lax.fori_loop(0, steps, step, (zero,) * (SUB * group), unroll=unroll)
            for g in range(group):
                store(table, row + g * SUB, col, accs[g::group])
            return carry

        lax.fori_loop(0, (rows // SUB) * (rows // SUB // group), pair_block, 0)

    pair_table(0, first, middle)
    pair_table(2, middle, last)


def partial_tables(roles, pivots, own, near, far):
    rows, width = own.shape
    count = pivots.shape[0]
    smem = pl.BlockSpec(memory_space=pltpu.SMEM)
    hbm = pl.BlockSpec(memory_space=pl.ANY)
    pairs = (3 + count) * rows * rows * width
    return pl.pallas_call(
        functools.partial(table_kernel, min(UNROLL, width // LANES)),
        out_shape=jax.ShapeDtypeStruct((3 + count, rows, rows), jnp.float32),
        in_specs=[smem, smem, hbm, hbm, hbm],
        out_specs=pl.BlockSpec(memory_space=pltpu.VMEM),
        scratch_shapes=[
            pltpu.VMEM((3, rows, width), jnp.float32),
            pltpu.VMEM((count, SUB, width), jnp.float32),
            pltpu.SemaphoreType.DMA((3,)),
        ],
        compiler_params=pltpu.CompilerParams(vmem_limit_bytes=40 << 20),
        cost_estimate=pl.CostEstimate(
            flops=2 * pairs, bytes_accessed=3 * rows * width * 4, transcendentals=0
        ),
    )(roles, pivots, own, near, far)


def body(profiles, pivots, roles):
    stride = lax.axis_size("vec") // 8
    n = lax.axis_size("fld")
    width, fields = profiles.shape
    count_piv = pivots.shape[1]
    row_count = width // n
    chosen = pivots[0]
    cut = max(fields // (FIRST * LANES), 1) * LANES
    spans = ((0, cut), (cut, fields)) if cut < fields else ((0, fields),)
    tables = None
    owned, arrived = [], []
    for begin, end in spans:
        own = profiles[:, begin:end]
        if arrived:
            own, *arrived[-1] = lax.optimization_barrier((own, *arrived[-1]))
        arrived.append([shifted(own, "vec", stride), shifted(own, "vec", 2 * stride)])
        owned.append(own)
    for own, (near, far) in zip(owned, arrived):
        part = partial_tables(roles[0], chosen, own, near, far)
        tables = part if tables is None else tables + part

    pivot_part = jnp.take(tables[2], chosen, axis=0)
    me = lax.axis_index("fld")
    total = None
    for by in range(n):
        start = lax.rem(me + by, n) * row_count
        piece = lax.dynamic_slice_in_dim(tables, start, row_count, axis=1)
        piece = piece.reshape((3 + count_piv) * row_count, width)
        piece = jnp.concatenate([piece, pivot_part], 0)
        if by:
            piece = shifted(piece, "fld", by)
        total = piece if total is None else total + piece
    total = total * (1.0 / FIELDS)
    rows = total[: (3 + count_piv) * row_count].reshape(3 + count_piv, row_count, width)
    pivot_rows = total[(3 + count_piv) * row_count :]
    first_cols = jnp.take(rows[0], chosen, axis=1)
    pair_tables = jnp.transpose(rows[:3], (1, 0, 2))
    triple = jnp.transpose(rows[3:], (1, 0, 2))
    similar = (
        first_cols[:, :, None] + pair_tables[:, 1, :][:, None, :] + pivot_rows[None, :, :] - triple
    ) * 0.5
    return (pair_tables[None], similar[None])


def solution(mesh):
    return jax.shard_map(
        body,
        mesh=mesh,
        in_specs=(P("vec", "fld"), P("vec", None), P("vec", None)),
        out_specs=(P("vec", "fld", None, None), P("vec", "fld", None, None)),
        check_vma=False,
    )
```

```python
import functools

import jax
import jax.numpy as jnp
from jax import lax
from jax.experimental import pallas as pl
from jax.experimental.pallas import tpu as pltpu
from jax.sharding import PartitionSpec as P

FIELDS = 32768
FIRST = 4
LANES = 128
SUB = 8
TRIPLE_COLS = 8
PAIR_ROWS = 4
UNROLL = 24


def shifted(shard, axis, by):
    peers = lax.axis_size(axis)
    return lax.ppermute(shard, axis, [(i, (i + by) % peers) for i in range(peers)])


def table_kernel(unroll, roles, pivots, own, near, far, out, held, piv, sems):
    rows, width = own.shape
    count = piv.shape[0]
    steps = width // LANES
    copies = [
        pltpu.make_async_copy(block, held.at[i], sems.at[i])
        for i, block in enumerate((own, near, far))
    ]
    for copy in copies:
        copy.start()
    for copy in copies:
        copy.wait()
    first, middle, last = roles[0], roles[1], roles[2]

    def tile(which, row, col):
        return held[which, pl.ds(pl.multiple_of(row, SUB), SUB), pl.ds(pl.multiple_of(col, LANES), LANES)]

    sub_id = lax.broadcasted_iota(jnp.int32, (SUB, LANES), 0)
    lane_id = lax.broadcasted_iota(jnp.int32, (SUB, LANES), 1)
    for m in range(count):
        base = (pivots[m] // SUB) * SUB
        keep = sub_id == pivots[m] - base

        def spread(step, carry, m=m, base=base, keep=keep):
            col = step * LANES
            value = jnp.sum(jnp.where(keep, tile(middle, base, col), 0.0), axis=0, keepdims=True)
            piv[m, :, pl.ds(pl.multiple_of(col, LANES), LANES)] = jnp.broadcast_to(value, (SUB, LANES))
            return carry

        lax.fori_loop(0, steps, spread, 0)

    def store(table, row, col, sums):
        where = pl.ds(pl.multiple_of(row, SUB), SUB)
        current = out[table, where, :]
        for j, acc in enumerate(sums):
            total = jnp.sum(acc, axis=1, keepdims=True)
            current = jnp.where(lane_id == col + j, total, current)
        out[table, where, :] = current

    def triple_block(index, carry):
        row = (index // (rows // SUB)) * SUB
        col = (index % (rows // SUB)) * SUB
        for half in range(0, SUB, TRIPLE_COLS):

            def step(k, accs, half=half):
                at = k * LANES
                lead = tile(first, row, at)
                tail = tile(last, col, at)
                points = [piv[m, :, pl.ds(pl.multiple_of(at, LANES), LANES)] for m in range(count)]
                new = []
                for j in range(TRIPLE_COLS):
                    end = tail[half + j : half + j + 1]
                    both = jnp.minimum(lead, jnp.broadcast_to(end, (SUB, LANES)))
                    new.append(accs[j * (count + 1)] + both)
                    for m in range(count):
                        new.append(accs[j * (count + 1) + 1 + m] + jnp.minimum(both, points[m]))
                return tuple(new)

            zero = jnp.zeros((SUB, LANES), jnp.float32)
            accs = lax.fori_loop(0, steps, step, (zero,) * (TRIPLE_COLS * (count + 1)), unroll=unroll)
            store(1, row, col + half, accs[0 :: count + 1])
            for m in range(count):
                store(3 + m, row, col + half, accs[1 + m :: count + 1])
        return carry

    lax.fori_loop(0, (rows // SUB) ** 2, triple_block, 0)

    def pair_table(table, left, right):
        group = PAIR_ROWS if rows % (PAIR_ROWS * SUB) == 0 else 1

        def pair_block(index, carry):
            row = (index // (rows // SUB)) * SUB * group
            col = (index % (rows // SUB)) * SUB

            def step(k, accs):
                at = k * LANES
                leads = [tile(left, row + g * SUB, at) for g in range(group)]
                tail = tile(right, col, at)
                new = []
                for j in range(SUB):
                    spread = jnp.broadcast_to(tail[j : j + 1], (SUB, LANES))
                    for g in range(group):
                        new.append(accs[j * group + g] + jnp.minimum(leads[g], spread))
                return tuple(new)

            zero = jnp.zeros((SUB, LANES), jnp.float32)
            accs = lax.fori_loop(0, steps, step, (zero,) * (SUB * group), unroll=unroll)
            for g in range(group):
                store(table, row + g * SUB, col, accs[g::group])
            return carry

        lax.fori_loop(0, (rows // SUB) * (rows // SUB // group), pair_block, 0)

    pair_table(0, first, middle)
    pair_table(2, middle, last)


def partial_tables(roles, pivots, own, near, far):
    rows, width = own.shape
    count = pivots.shape[0]
    smem = pl.BlockSpec(memory_space=pltpu.SMEM)
    hbm = pl.BlockSpec(memory_space=pl.ANY)
    pairs = (3 + count) * rows * rows * width
    return pl.pallas_call(
        functools.partial(table_kernel, min(UNROLL, width // LANES)),
        out_shape=jax.ShapeDtypeStruct((3 + count, rows, rows), jnp.float32),
        in_specs=[smem, smem, hbm, hbm, hbm],
        out_specs=pl.BlockSpec(memory_space=pltpu.VMEM),
        scratch_shapes=[
            pltpu.VMEM((3, rows, width), jnp.float32),
            pltpu.VMEM((count, SUB, width), jnp.float32),
            pltpu.SemaphoreType.DMA((3,)),
        ],
        compiler_params=pltpu.CompilerParams(vmem_limit_bytes=40 << 20),
        cost_estimate=pl.CostEstimate(
            flops=2 * pairs, bytes_accessed=3 * rows * width * 4, transcendentals=0
        ),
    )(roles, pivots, own, near, far)


def body(profiles, pivots, roles):
    stride = lax.axis_size("vec") // 8
    n = lax.axis_size("fld")
    width, fields = profiles.shape
    count_piv = pivots.shape[1]
    row_count = width // n
    chosen = pivots[0]
    cut = max(fields // (FIRST * LANES), 1) * LANES
    spans = ((0, cut), (cut, fields)) if cut < fields else ((0, fields),)
    tables = None
    owned, arrived = [], []
    for begin, end in spans:
        own = profiles[:, begin:end]
        if arrived:
            own, *arrived[-1] = lax.optimization_barrier((own, *arrived[-1]))
        arrived.append([shifted(own, "vec", stride), shifted(own, "vec", 2 * stride)])
        owned.append(own)
    for own, (near, far) in zip(owned, arrived):
        part = partial_tables(roles[0], chosen, own, near, far)
        tables = part if tables is None else tables + part

    pivot_part = jnp.take(tables[2], chosen, axis=0)
    me = lax.axis_index("fld")
    total = None
    for by in range(n):
        start = lax.rem(me + by, n) * row_count
        piece = lax.dynamic_slice_in_dim(tables, start, row_count, axis=1)
        piece = piece.reshape((3 + count_piv) * row_count, width)
        piece = jnp.concatenate([piece, pivot_part], 0)
        if by:
            piece = shifted(piece, "fld", by)
        total = piece if total is None else total + piece
    total = total * (1.0 / FIELDS)
    rows = total[: (3 + count_piv) * row_count].reshape(3 + count_piv, row_count, width)
    pivot_rows = total[(3 + count_piv) * row_count :]
    first_cols = jnp.take(rows[0], chosen, axis=1)
    pair_tables = jnp.transpose(rows[:3], (1, 0, 2))
    triple = jnp.transpose(rows[3:], (1, 0, 2))
    similar = (
        first_cols[:, :, None] + pair_tables[:, 1, :][:, None, :] + pivot_rows[None, :, :] - triple
    ) * 0.5
    return (pair_tables[None], similar[None])


def solution(mesh):
    return jax.shard_map(
        body,
        mesh=mesh,
        in_specs=(P("vec", "fld"), P("vec", None), P("vec", None)),
        out_specs=(P("vec", "fld", None, None), P("vec", "fld", None, None)),
        check_vma=False,
    )
```
